32 devices in a mesh: dp: 16 (over z, y, x), tensor: 2 (over core).
Axes of the slice: x: 2, y: 2, z: 4, core: 2. Of those that a mesh axis runs over, the one named last changes fastest.
Arguments:
- layer_input: bfloat16 [32, 1024, 768], P(('dp', 'tensor')), may hold values from -6 to 6
- lengths: int32 [32], P('dp'), may hold values from 100 to 1024, as said below
- predicted: int32 [32, 1024], P(('dp', 'tensor')), may hold values from 0 to 69
- w_qkv: bfloat16 [3, 768, 768], P(None, None, 'tensor'), may hold values from -0.21875 to 0.21875
- b_qkv: bfloat16 [3, 768], P(None, 'tensor'), may hold values from -3 to 3
- w_out: bfloat16 [768, 768], P('tensor'), may hold values from -1.75 to 1.75
- b_out: bfloat16 [768], replicated, may hold values from -2 to 2
- w_up: bfloat16 [768, 3072], P(None, 'tensor'), may hold values from -0.21875 to 0.21875
- b_up: bfloat16 [3072], P('tensor'), may hold values from -3 to 3
- w_down: bfloat16 [3072, 768], P('tensor'), may hold values from -0.109375 to 0.109375
- b_down: bfloat16 [768], replicated, may hold values from -2 to 2
- first_gain: bfloat16 [768], replicated, may hold values from 0.099609375 to 1.8984375
- first_bias: bfloat16 [768], replicated, may hold values from -2 to 2
- second_gain: bfloat16 [768], replicated, may hold values from 0.099609375 to 1.8984375
- second_bias: bfloat16 [768], replicated, may hold values from -2 to 2
- cotangent: bfloat16 [32, 1024, 768], P(('dp', 'tensor')), may hold values from -6 to 6
Outputs:
- layer_output: bfloat16 [32, 1024, 768], P(('dp', 'tensor'))
- input_grad: bfloat16 [32, 1024, 768], P(('dp', 'tensor'))
- grad_w_qkv: float32 [3, 768, 768], P(None, None, 'tensor')
- grad_b_qkv: float32 [3, 768], P(None, 'tensor')
- grad_w_out: float32 [768, 768], P('tensor')
- grad_b_out: float32 [768], replicated
- grad_w_up: float32 [768, 3072], P(None, 'tensor')
- grad_b_up: float32 [3072], P('tensor')
- grad_w_down: float32 [3072, 768], P('tensor')
- grad_b_down: float32 [768], replicated
- grad_first_gain: float32 [768], replicated
- grad_first_bias: float32 [768], replicated
- grad_second_gain: float32 [768], replicated
- grad_second_bias: float32 [768], replicated
- codon_rate: float32 [70], replicated
The draws below stay inside these ranges and needn't reach their ends.
Inputs may be any that keep to these rules, and one draw needn't show every extreme that they name: `lengths`: a sequence holds its real codons at positions below its length and padding after; the first sequence has 1024 codons. `predicted`: padded positions hold classes as well.
All inputs are finite; a program needn't handle non-finite values.
Results may differ from the reference program's by a relative error of at most 0.015.
Values may be sent and summed in bfloat16 or wider, within the bound.
No kernel may reach another device: no remote copies, remote signals or barrier semaphores. Data moves between devices by JAX's collectives and lax.ppermute only.
A program may use at most 256 MiB of HBM per device.

```python
import math
import jax
import jax.numpy as jnp
import numpy as np
from jax import lax

D = 768
HEADS = 12
HEAD_DIM = 64
FF = 3072
CLASSES = 70
LEN = 1024
MINLEN = 100
SEQS = 32


def draw_lengths(key, part):
    span = LEN - MINLEN
    raw = jax.random.randint(key, (SEQS,), 0, span + 1)
    shorter = MINLEN + (raw * raw + 2 * raw * span) // (3 * span)
    first = jnp.arange(SEQS) == 0
    return jnp.where(first, LEN, shorter).astype(jnp.int32)


def place_ends(entries, own_key, smallest, top_value):
    longest = entries.shape.index(max(entries.shape))
    spots = []
    for shift in (0, 1):
        where = [jax.random.randint(jax.random.fold_in(own_key, axis), (), 0, length) for axis, length in enumerate(entries.shape)]
        where[longest] = (where[longest] + shift) % entries.shape[longest]
        spots.append(tuple(where))
    return entries.at[spots[0]].set(smallest).at[spots[1]].set(top_value)


def block_scale(stream_key, extent, shards, least, high):
    def one(axis_at, shards_of):
        heights = jax.random.uniform(jax.random.fold_in(jax.random.fold_in(stream_key, 6), axis_at), (shards_of,), jnp.float32, least / len(shards), high / len(shards))
        return jnp.repeat(jnp.exp(heights), extent[axis_at] // shards_of).reshape((-1,) + (1,) * (len(extent) - axis_at - 1))

    level = one(*shards[0])
    for cut in shards[1:]:
        level = level * one(*cut)
    return level


def cumulative_ranks(amount, skew):
    portions = [(1 << 20) // math.isqrt(rank ** skew) + 1 for rank in range(1, amount + 1)]
    deviation = 1 + sum(portions) // (1 << 30)
    return np.cumsum(np.array([max(1, weight // deviation) for weight in portions]))


def skewed_ids(key, shape, number_of, lean):
    grid = cumulative_ranks(number_of, lean)
    ticket = jax.random.randint(jax.random.fold_in(key, 1), shape, 0, int(grid[number_of - 1]))
    rank = jnp.searchsorted(jnp.asarray(grid, jnp.int32), ticket, side="right")
    return jax.random.permutation(jax.random.fold_in(key, 2), number_of)[rank].astype(jnp.int32)


def gaussian(stream_key, extent, deviation, reach, pieces=(), dtype=jnp.bfloat16):
    array = jax.random.normal(stream_key, extent, jnp.float32) * deviation
    if len(pieces) > 0:
        array = block_scale(stream_key, extent, pieces, -0.22, 0.18) * array
    return jnp.clip(array, min=-reach, max=reach).astype(dtype)


def setup_inputs(seed: int = 0) -> dict:
    splits = jax.random.split(jax.random.key(seed), 17)
    layer_input = gaussian(splits[0], (SEQS, LEN, D), 1.0, 6.0, ((0, 32),))
    lengths = draw_lengths(jax.random.fold_in(splits[16], 71), 0)
    predicted = place_ends(skewed_ids(splits[2], (SEQS, LEN), CLASSES, 2), jax.random.fold_in(splits[2], 3), 0, CLASSES - 1).astype(jnp.int32)
    w_qkv = gaussian(splits[3], (3, D, D), D ** -0.5, 0.21875, ((2, 2),))
    b_qkv = gaussian(splits[4], (3, D), 0.5, 3.0, ((1, 2),))
    w_out = gaussian(splits[5], (D, D), (D // 64) ** -0.5, 1.75, ((0, 2),))
    b_out = gaussian(splits[6], (D,), 0.3, 2.0)
    w_up = gaussian(splits[7], (D, FF), D ** -0.5, 0.21875, ((1, 2),))
    b_up = gaussian(splits[8], (FF,), 0.5, 3.0, ((0, 2),))
    w_down = gaussian(splits[9], (FF, D), FF ** -0.5, 0.109375, ((0, 2),))
    b_down = gaussian(splits[10], (D,), 0.3, 2.0)
    first_gain = jnp.clip(1.0 + 0.18 * jax.random.normal(splits[11], (D,), jnp.float32), 0.099609375, 1.8984375).astype(jnp.bfloat16)
    first_bias = gaussian(splits[12], (D,), 0.3, 2.0)
    second_gain = jnp.clip(1.0 + 0.18 * jax.random.normal(splits[13], (D,), jnp.float32), 0.099609375, 1.8984375).astype(jnp.bfloat16)
    second_bias = gaussian(splits[14], (D,), 0.3, 2.0)
    cotangent = gaussian(splits[15], (SEQS, LEN, D), 1.0, 6.0, ((0, 32),))
    return dict(layer_input=layer_input, lengths=lengths, predicted=predicted, w_qkv=w_qkv, b_qkv=b_qkv, w_out=w_out, b_out=b_out, w_up=w_up, b_up=b_up, w_down=w_down, b_down=b_down, first_gain=first_gain, first_bias=first_bias, second_gain=second_gain, second_bias=second_bias, cotangent=cotangent)


EPSILON = 1e-05
PRECISE = lax.Precision.HIGHEST

@jax.custom_vjp
def low(v):
    return lax.optimization_barrier(v.astype(jnp.bfloat16)).astype(jnp.float32)

@jax.custom_vjp
def low_back(v):
    return v

def low_keep(v):
    return (low(v), None)

def low_pass(kept, grad):
    return (grad,)

def back_keep(v):
    return (v, None)

def back_low(kept, grad):
    return (low(grad),)
low.defvjp(low_keep, low_pass)
low_back.defvjp(back_keep, back_low)

def norm_layer(inputs, gain_vec, shift_vec):
    row_mean = lax.optimization_barrier(jnp.mean(inputs, axis=-1, keepdims=True))
    centred = inputs - row_mean
    variance = lax.optimization_barrier(jnp.mean(centred * centred, axis=-1, keepdims=True))
    return centred * lax.rsqrt(variance + EPSILON) * gain_vec + shift_vec

def rotary_tables(seq_len, head_size):
    half_dim = head_size // 2
    frequency = 10000.0 ** (-2.0 * jnp.arange(half_dim).astype(jnp.float32) / head_size)
    angles = jnp.arange(seq_len).astype(jnp.float32)[:, None] * frequency[None, :]
    angles = jnp.concatenate([angles, angles], axis=1)
    return (jnp.cos(angles), jnp.sin(angles))

def rotate(inputs, cosine_table, sine_table):
    half_dim = inputs.shape[-1] // 2
    turned = jnp.concatenate([-inputs[..., half_dim:], inputs[..., :half_dim]], axis=-1)
    return inputs * cosine_table[:, None, :] + turned * sine_table[:, None, :]

def block(inputs, seq_lengths, params):
    w_qkv, b_qkv, w_out, b_out, w_up, b_up, w_down, b_down, first_gain, first_bias, second_gain, second_bias = params
    seq_count = inputs.shape[0]
    cosine_table, sine_table = rotary_tables(LEN, HEAD_DIM)
    normed = low(norm_layer(inputs, first_gain, first_bias))
    projected = jnp.einsum('bld,cde->cble', normed, w_qkv, precision=PRECISE) + b_qkv[:, None, None, :]
    projected = low_back(projected).reshape(3, seq_count, LEN, HEADS, HEAD_DIM)
    queries = low(rotate(projected[0], cosine_table, sine_table))
    keys_rot = low(rotate(projected[1], cosine_table, sine_table))
    values = low(projected[2])
    scores = jnp.einsum('bqhd,bkhd->bhqk', queries, keys_rot, precision=PRECISE) * HEAD_DIM ** (-0.5)
    key_valid = jnp.arange(LEN)[None, :] < seq_lengths[:, None]
    scores = low_back(jnp.where(key_valid[:, None, None, :], scores, -1000000000.0))
    prob_low = low(jax.nn.softmax(scores, axis=-1))
    mixed_heads = jnp.einsum('bhqk,bkhd->bqhd', prob_low, values, precision=PRECISE).reshape(seq_count, LEN, D)
    mixed_heads = low(low_back(mixed_heads))
    attention = low_back(jnp.einsum('ble,ed->bld', mixed_heads, w_out, precision=PRECISE) + b_out)
    residual = inputs + attention
    normed_two = low(norm_layer(residual, second_gain, second_bias))
    up_proj = low_back(jnp.einsum('bld,df->blf', normed_two, w_up, precision=PRECISE) + b_up)
    activation = low(jax.nn.gelu(up_proj, approximate=False))
    feed_forward = low_back(jnp.einsum('blf,fd->bld', activation, w_down, precision=PRECISE) + b_down)
    return residual + feed_forward

def reference(layer_input, lengths, predicted, w_qkv, b_qkv, w_out, b_out, w_up, b_up, w_down, b_down, first_gain, first_bias, second_gain, second_bias, cotangent):
    params = tuple((weight_arg.astype(jnp.float32) for weight_arg in (w_qkv, b_qkv, w_out, b_out, w_up, b_up, w_down, b_down, first_gain, first_bias, second_gain, second_bias)))
    group_count = SEQS // 4
    grouped_lengths = lengths.reshape(group_count, 4)

    def forward(inputs, *weights):
        grouped = inputs.reshape(group_count, 4, LEN, D)
        run_group = jax.checkpoint(lambda pair: block(pair[0], pair[1], weights))
        outputs = lax.map(run_group, (grouped, grouped_lengths))
        return outputs.reshape(SEQS, LEN, D)
    result, pull_back = jax.vjp(forward, layer_input.astype(jnp.float32), *params)
    gradients = pull_back(cotangent.astype(jnp.float32))
    classes = jnp.arange(CLASSES)
    valid_pos = jnp.arange(LEN)[None, :] < lengths[:, None]
    class_hits = jnp.where((predicted[None, :, :] == classes[:, None, None]) & valid_pos[None, :, :], jnp.float32(1.0), jnp.float32(0.0))
    codon_rate = lax.optimization_barrier(jnp.sum(class_hits, axis=(1, 2))) * (CLASSES / (SEQS * LEN))
    return (result.astype(jnp.bfloat16), gradients[0].astype(jnp.bfloat16), gradients[1], gradients[2], gradients[3], gradients[4], gradients[5], gradients[6], gradients[7], gradients[8], gradients[9], gradients[10], gradients[11], gradients[12], codon_rate)
```

```python
import functools

import jax
import jax.numpy as jnp
import numpy as np
from jax import lax
from jax.experimental import pallas as pl
from jax.experimental.pallas import tpu as pltpu
from jax.sharding import PartitionSpec as P

HEAD_DIM = 64
CLASSES = 70
EPSILON = 1e-05
PAIR = 2 * HEAD_DIM
BF = jnp.bfloat16
F32 = jnp.float32
NN = (((1,), (0,)), ((), ()))
NT = (((1,), (1,)), ((), ()))
VMEM_LIMIT = 60 * 1024 * 1024

ERF_P = 0.39
ERF_C = (
    0.2353350342991649,
    0.09132489362337098,
    0.6497226730753285,
    -0.6356086817390623,
    0.886796488962974,
    -0.22757041290383279,
)


def dot(a, b, dims):
    return lax.dot_general(a, b, dims, preferred_element_type=F32)


def call(body, grid, in_specs, out_specs, out_shape, flops, nbytes, scratch=(), name=None):
    return pl.pallas_call(
        body,
        grid=grid,
        in_specs=in_specs,
        out_specs=out_specs,
        out_shape=out_shape,
        scratch_shapes=list(scratch),
        compiler_params=pltpu.CompilerParams(vmem_limit_bytes=VMEM_LIMIT),
        cost_estimate=pl.CostEstimate(
            flops=int(flops), bytes_accessed=int(nbytes), transcendentals=0
        ),
        name=name,
    )


def rope_tables(length):
    half = HEAD_DIM // 2
    freq = np.float32(10000.0) ** (-2.0 * np.arange(half).astype(np.float32) / np.float32(HEAD_DIM))
    angles = np.arange(length).astype(np.float32)[:, None] * freq.astype(np.float32)[None, :]
    cosine = np.cos(angles)
    sine = np.sin(angles)
    cosine = np.concatenate([cosine, cosine, cosine, cosine], axis=1)
    sine = np.concatenate([-sine, sine, -sine, sine], axis=1)
    return cosine.astype(np.float32), sine.astype(np.float32)


def turn(v):
    lane = lax.broadcasted_iota(jnp.int32, v.shape, 1)
    first = lax.rem(lane, HEAD_DIM) < HEAD_DIM // 2
    half = HEAD_DIM // 2
    return jnp.where(first, pltpu.roll(v, PAIR - half, 1), pltpu.roll(v, half, 1))


def ln_forward(x):
    centred = x - jnp.mean(x, axis=-1, keepdims=True)
    scale = lax.rsqrt(jnp.mean(centred * centred, axis=-1, keepdims=True) + EPSILON)
    return centred * scale, scale


def ln_backward(xhat, scale, grad, gain):
    h = grad * gain
    mean_h = jnp.mean(h, axis=-1, keepdims=True)
    mean_hx = jnp.mean(h * xhat, axis=-1, keepdims=True)
    return scale * (h - mean_h - xhat * mean_hx)


def full(shape):
    zeros = (0,) * len(shape)
    return pl.BlockSpec(shape, lambda *_: zeros)


def project_body(normalize, *refs):
    if normalize:
        x_ref, g_ref, b_ref, w_ref, bias_ref, cos_ref, sin_ref, n_ref, q_ref, k_ref, v_ref = refs
        xhat, _ = ln_forward(x_ref[...].astype(F32))
        normed = (xhat * g_ref[...] + b_ref[...]).astype(BF)
        n_ref[...] = normed
    else:
        n_ref, w_ref, bias_ref, cos_ref, sin_ref, q_ref, k_ref, v_ref = refs
        normed = n_ref[...]
    cosine, sine = cos_ref[...], sin_ref[...]
    width = w_ref.shape[2]
    for c, out in ((0, q_ref), (1, k_ref), (2, v_ref)):
        y = dot(normed, w_ref[c], NN) + bias_ref[c : c + 1, :]
        if c == 2:
            out[...] = y.astype(BF)
            continue
        for p in range(width // PAIR):
            piece = y[:, p * PAIR : (p + 1) * PAIR]
            piece = piece * cosine + turn(piece) * sine
            if c == 0:
                piece = piece * (HEAD_DIM**-0.5)
            out[:, p * PAIR : (p + 1) * PAIR] = piece.astype(BF)


def project(x, gain, bias, w, b, cosine, sine, normalize):
    length, width = x.shape
    half = w.shape[2]
    rows = 256
    row = lambda n: pl.BlockSpec((rows, n), lambda i: (i, 0))
    head = [x, gain, bias] if normalize else [x]
    head_specs = [row(width)] + ([full((1, width))] * 2 if normalize else [])
    outs = [jax.ShapeDtypeStruct((length, half), BF)] * 3
    out_specs = [row(half)] * 3
    if normalize:
        outs = [jax.ShapeDtypeStruct((length, width), BF)] + outs
        out_specs = [row(width)] + out_specs
    return call(
        functools.partial(project_body, normalize),
        (length // rows,),
        head_specs + [full(w.shape), full(b.shape), row(PAIR), row(PAIR)],
        out_specs,
        outs,
        2 * length * width * half * 3,
        2 * (length * width * 2 + 3 * width * half + 3 * length * half),
        name="project",
    )(*head, w, b, cosine, sine)


def attend_body(len_ref, q_ref, k_ref, v_ref, e_ref, ot_ref, o_ref, linv_ref):
    length = q_ref.shape[0]
    step = 256
    valid = lax.broadcasted_iota(jnp.int32, (length, PAIR), 0) < len_ref[0]
    lane = lax.broadcasted_iota(jnp.int32, (length, PAIR), 1)
    q, k = q_ref[...], k_ref[...]
    v_t = jnp.transpose(v_ref[...])
    ones = jnp.ones((16, length), BF)
    mask = jnp.where(valid, 0.0, -1.0e9).astype(BF)
    work = []
    for h in range(2):
        other = HEAD_DIM * (1 - h)
        own = (lane >= HEAD_DIM * h) & (lane < HEAD_DIM * (h + 1))
        q_h = jnp.where(own, q, jnp.where(lane == other, 1.0, 0.0).astype(BF))
        k_h = jnp.where(lane == other, mask, k)
        v_h = jnp.concatenate([v_t[HEAD_DIM * h : HEAD_DIM * (h + 1)], ones], axis=0)
        for c in range(length // step):
            work.append((h, c, q_h, k_h, v_h))

    def scores(item):
        h, c, q_h, k_h, v_h = item
        return dot(k_h, q_h[c * step : (c + 1) * step], NT)

    ahead = scores(work[0])
    for i, item in enumerate(work):
        h, c, q_h, k_h, v_h = item
        now = ahead
        if i + 1 < len(work):
            ahead = scores(work[i + 1])
        where = slice(c * step, (c + 1) * step)
        top = jnp.max(now, axis=0, keepdims=True)
        e = jnp.exp(now - top).astype(BF)
        e_ref[h, :, where] = e
        o = dot(v_h, e, NN)
        linv = 1.0 / o[HEAD_DIM : HEAD_DIM + 1]
        linv_ref[0, h : h + 1, where] = linv
        ot_ref[HEAD_DIM * h : HEAD_DIM * (h + 1), where] = (o[:HEAD_DIM] * linv).astype(BF)
    o_ref[...] = jnp.transpose(ot_ref[...])


def attend(own_length, q, k, v):
    length, half = q.shape
    pairs = half // PAIR
    col = pl.BlockSpec((length, PAIR), lambda p: (0, p))
    return call(
        attend_body,
        (pairs,),
        [pl.BlockSpec(memory_space=pltpu.SMEM), col, col, col],
        [
            pl.BlockSpec((2, length, length), lambda p: (p, 0, 0)),
            pl.BlockSpec((PAIR, length), lambda p: (p, 0)),
            col,
            pl.BlockSpec((1, 8, length), lambda p: (p, 0, 0)),
        ],
        [
            jax.ShapeDtypeStruct((2 * pairs, length, length), BF),
            jax.ShapeDtypeStruct((half, length), BF),
            jax.ShapeDtypeStruct((length, half), BF),
            jax.ShapeDtypeStruct((pairs, 8, length), F32),
        ],
        2 * 4 * length * length * PAIR * pairs,
        4 * pairs * length * length,
        name="attend",
    )(own_length, q, k, v)


def attend_grad_body(
    e_ref, linv_ref, q_ref, k_ref, v_ref, ot_ref, dot_ref, cos_ref, sin_ref, dq_ref, dk_ref, dv_ref
):
    length = q_ref.shape[0]
    step = 256
    lane = lax.broadcasted_iota(jnp.int32, (length, PAIR), 1)
    q, v = q_ref[...], v_ref[...]
    k_t = jnp.transpose(k_ref[...])
    zeros = jnp.zeros((HEAD_DIM, length), BF)
    work = []
    for h in range(2):
        rows = slice(HEAD_DIM * h, HEAD_DIM * (h + 1))
        own = (lane >= HEAD_DIM * h) & (lane < HEAD_DIM * (h + 1))
        q_h = jnp.where(own, q, jnp.zeros_like(q))
        d_o = dot_ref[rows, :].astype(F32) * linv_ref[0, h : h + 1, :]
        delta = jnp.sum(d_o * ot_ref[rows, :].astype(F32), axis=0, keepdims=True)
        d_low = d_o.astype(BF)
        d_pad = jnp.concatenate([d_low, zeros] if h == 0 else [zeros, d_low], axis=0)
        for c in range(length // step):
            work.append((h, c, q_h, d_pad, delta, k_t[rows]))

    def grad_probs(item):
        h, c, q_h, d_pad, delta, k_h = item
        return dot(v, d_pad[:, c * step : (c + 1) * step], NN)

    d_v = jnp.zeros((length, PAIR), F32)
    d_k = jnp.zeros((length, PAIR), F32)
    d_q = [[], []]
    ahead = grad_probs(work[0])
    for i, item in enumerate(work):
        h, c, q_h, d_pad, delta, k_h = item
        now = ahead
        if i + 1 < len(work):
            ahead = grad_probs(work[i + 1])
        where = slice(c * step, (c + 1) * step)
        e = e_ref[h, :, where]
        d_s = (e.astype(F32) * (now - delta[:, where])).astype(BF)
        d_v = d_v + dot(e, d_pad[:, where], NT)
        d_k = d_k + dot(d_s, q_h[where], NN)
        d_q[h].append(dot(k_h, d_s, NN))
    cosine, sine = cos_ref[...], sin_ref[...]
    dv_ref[...] = d_v.astype(BF)
    dk_ref[...] = (d_k * cosine - turn(d_k) * sine).astype(BF)
    both = [jnp.concatenate(parts, axis=1) for parts in d_q]
    both = jnp.transpose(jnp.concatenate(both, axis=0)) * (HEAD_DIM**-0.5)
    dq_ref[...] = (both * cosine - turn(both) * sine).astype(BF)


def attend_grad(e, linv, q, k, v, o_t, do_t, cosine, sine):
    length, half = q.shape
    pairs = half // PAIR
    col = pl.BlockSpec((length, PAIR), lambda p: (0, p))
    row = pl.BlockSpec((PAIR, length), lambda p: (p, 0))
    return call(
        attend_grad_body,
        (pairs,),
        [
            pl.BlockSpec((2, length, length), lambda p: (p, 0, 0)),
            pl.BlockSpec((1, 8, length), lambda p: (p, 0, 0)),
            col,
            col,
            col,
            row,
            row,
            full((length, PAIR)),
            full((length, PAIR)),
        ],
        [col] * 3,
        [jax.ShapeDtypeStruct((length, half), BF)] * 3,
        2 * 8 * length * length * PAIR * pairs,
        4 * pairs * length * length,
        name="attend_grad",
    )(e, linv, q, k, v, o_t, do_t, cosine, sine)


def out_body(o1_ref, o2_ref, w1_ref, w2_ref, x_ref, b_ref, g_ref, s_ref, res_ref, n_ref):
    res = dot(o1_ref[...], w1_ref[...], NN) + dot(o2_ref[...], w2_ref[...], NN)
    res = x_ref[...].astype(F32) + (res + b_ref[...])
    res_ref[...] = res
    xhat, _ = ln_forward(res)
    n_ref[...] = (xhat * g_ref[...] + s_ref[...]).astype(BF)


def out_project(o1, o2, w1, w2, x, b_out, gain, bias):
    length, width = x.shape
    half = w1.shape[0]
    rows = 256
    row = lambda n: pl.BlockSpec((rows, n), lambda i: (i, 0))
    return call(
        out_body,
        (length // rows,),
        [row(half), row(half), full(w1.shape), full(w2.shape), row(width)] + [full((1, width))] * 3,
        [row(width)] * 2,
        [jax.ShapeDtypeStruct((length, width), F32), jax.ShapeDtypeStruct((length, width), BF)],
        2 * length * width * half * 2,
        length * width * 10,
        name="out_project",
    )(o1, o2, w1, w2, x, b_out, gain, bias)


def gelu_parts(u):
    z = jnp.abs(u) * (0.5**0.5)
    t = 1.0 / (1.0 + ERF_P * z)
    poly = jnp.full_like(t, ERF_C[-1])
    for coef in ERF_C[-2::-1]:
        poly = poly * t + coef
    e = jnp.exp(u * u * -0.5)
    tail = 0.5 * (poly * t) * e
    cdf = jnp.where(u >= 0, 1.0 - tail, tail)
    return u * cdf, cdf + u * (e * 0.3989422804014327)


def mlp_body(last, *refs):
    if last:
        (n_ref, ct_ref, wu_ref, bu_ref, wd_ref, ff_in, dn_in, res_ref, bd_ref, g_ref) = refs[:10]
        (dwu_ref, dwd_ref, dbu_ref, y_ref, gres_ref, ga_ref, vec_ref, ff_ref, dn_ref, nt_ref) = refs[10:]
    else:
        n_ref, ct_ref, wu_ref, bu_ref, wd_ref = refs[:5]
        dwu_ref, dwd_ref, dbu_ref, ff_ref, dn_ref, nt_ref = refs[5:]
    j = pl.program_id(0)

    @pl.when(j == 0)
    def _():
        nt_ref[...] = jnp.transpose(n_ref[...])
        if last:
            ff_ref[...] = ff_in[...]
            dn_ref[...] = dn_in[...]
        else:
            ff_ref[...] = jnp.zeros_like(ff_ref)
            dn_ref[...] = jnp.zeros_like(dn_ref)

    n, ct, wu, wd = n_ref[...], ct_ref[...], wu_ref[...], wd_ref[...]
    up = dot(n, wu, NN) + bu_ref[...]
    d_act = dot(ct, wd, NT)
    act, slope = gelu_parts(up)
    act = act.astype(BF)
    d_up = (d_act * slope).astype(BF)
    ff_ref[...] += dot(act, wd, NN)
    dwd_ref[...] = dot(jnp.transpose(act), ct, NN).astype(BF)
    dwu_ref[...] = dot(nt_ref[...], d_up, NN).astype(BF)
    dn_ref[...] += dot(d_up, wu, NT)
    dbu_ref[...] = jnp.sum(d_up.astype(F32), axis=0, keepdims=True)

    if last:

        @pl.when(j == pl.num_programs(0) - 1)
        def _():
            length = n_ref.shape[0]
            step = 128
            vec_ref[...] = jnp.zeros_like(vec_ref)

            def tail(i, carry):
                at = pl.ds(pl.multiple_of(i * step, step), step)
                res = res_ref[at, :]
                y_ref[at, :] = (res + (ff_ref[at, :] + bd_ref[...])).astype(BF)
                xhat, scale = ln_forward(res)
                d_n = dn_ref[at, :]
                c = ct_ref[at, :].astype(F32)
                g_res = c + ln_backward(xhat, scale, d_n, g_ref[...])
                gres_ref[at, :] = g_res
                low = g_res.astype(BF)
                ga_ref[at, :] = low
                vec_ref[0:1, :] += jnp.sum(d_n * xhat, axis=0, keepdims=True)
                vec_ref[1:2, :] += jnp.sum(d_n, axis=0, keepdims=True)
                vec_ref[2:3, :] += jnp.sum(low.astype(F32), axis=0, keepdims=True)
                vec_ref[3:4, :] += jnp.sum(c, axis=0, keepdims=True)
                return carry

            lax.fori_loop(0, length // step, tail, 0)


def mlp(n, ct, wu, bu, wd, rest=None):
    length, width = n.shape
    half = wu.shape[1]
    block = 512
    last = rest is not None
    whole = full((length, width))
    grad_specs = [
        pl.BlockSpec((width, block), lambda j: (0, j)),
        pl.BlockSpec((block, width), lambda j: (j, 0)),
        pl.BlockSpec((1, block), lambda j: (0, j)),
    ]
    in_specs = [
        whole,
        whole,
        grad_specs[0],
        grad_specs[2],
        grad_specs[1],
    ]
    args = [n, ct, wu, bu, wd]
    outs = [
        jax.ShapeDtypeStruct((width, half), BF),
        jax.ShapeDtypeStruct((half, width), BF),
        jax.ShapeDtypeStruct((1, half), F32),
    ]
    out_specs = list(grad_specs)
    big = jax.ShapeDtypeStruct((length, width), F32)
    low = jax.ShapeDtypeStruct((length, width), BF)
    scratch = [pltpu.VMEM((width, length), BF)]
    if last:
        args += list(rest)
        in_specs += [whole, whole, whole, full((1, width)), full((1, width))]
        outs += [low, big, low, jax.ShapeDtypeStruct((8, width), F32)]
        out_specs += [whole, whole, whole, full((8, width))]
        scratch = [pltpu.VMEM((length, width), F32)] * 2 + scratch
    else:
        outs += [big, big]
        out_specs += [whole, whole]
    return call(
        functools.partial(mlp_body, last),
        (half // block,),
        in_specs,
        out_specs,
        outs,
        2 * length * width * half * 6,
        length * width * 20 + 8 * width * half,
        scratch,
        name="mlp_last" if last else "mlp_first",
    )(*args)


def mixed_grad_body(w_ref, ot_ref, ga_ref, dm_ref, dw_ref):
    ga = ga_ref[...]
    dm_ref[...] = dot(w_ref[...], ga, NT).astype(BF)
    dw_ref[...] = dot(ot_ref[...], ga, NN).astype(BF)


def mixed_grad(w, o_t, ga):
    half, width = w.shape
    length = ga.shape[0]
    rows = PAIR
    row = lambda n: pl.BlockSpec((rows, n), lambda i: (i, 0))
    return call(
        mixed_grad_body,
        (half // rows,),
        [row(width), row(length), full(ga.shape)],
        [row(length), row(width)],
        [jax.ShapeDtypeStruct((half, length), BF), jax.ShapeDtypeStruct((half, width), BF)],
        4 * length * width * half,
        2 * (2 * half * length + length * width + 2 * half * width),
        name="mixed_grad",
    )(w, o_t, ga)


def weight_grad_body(n_ref, dq_ref, dk_ref, dv_ref, dw_ref, db_ref, nt_ref):
    nt_ref[...] = jnp.transpose(n_ref[...])
    for c, ref in enumerate((dq_ref, dk_ref, dv_ref)):
        d = ref[...]
        dw_ref[c] = dot(nt_ref[...], d, NN).astype(BF)
        db_ref[c : c + 1, :] = jnp.sum(d.astype(F32), axis=0, keepdims=True)


def weight_grad(n, grads):
    length, width = n.shape
    half = grads[0].shape[1]
    return call(
        weight_grad_body,
        (1,),
        [full(n.shape)] + [full((length, half))] * 3,
        [full((3, width, half)), full((3, half))],
        [jax.ShapeDtypeStruct((3, width, half), BF), jax.ShapeDtypeStruct((3, half), F32)],
        2 * length * width * half * 3,
        2 * (length * width + 3 * length * half + 3 * width * half),
        [pltpu.VMEM((width, length), BF)],
        name="weight_grad",
    )(n, *grads)


def input_grad_body(*refs):
    grads, (w1_ref, w2_ref, x_ref, gres_ref, g_ref), (out_ref, vec_ref) = (
        refs[:6],
        refs[6:11],
        refs[11:],
    )
    d_n = None
    for i, ref in enumerate(grads):
        term = dot(ref[...], (w1_ref if i < 3 else w2_ref)[i % 3], NT)
        d_n = term if d_n is None else d_n + term
    xhat, scale = ln_forward(x_ref[...].astype(F32))
    out_ref[...] = (gres_ref[...] + ln_backward(xhat, scale, d_n, g_ref[...])).astype(BF)

    @pl.when(pl.program_id(0) == 0)
    def _():
        vec_ref[...] = jnp.zeros_like(vec_ref)

    vec_ref[0:1, :] += jnp.sum(d_n * xhat, axis=0, keepdims=True)
    vec_ref[1:2, :] += jnp.sum(d_n, axis=0, keepdims=True)


def input_gradient(grads1, grads2, w1, w2, x, g_res, gain):
    length, width = x.shape
    half = grads1[0].shape[1]
    rows = 256
    row = lambda n: pl.BlockSpec((rows, n), lambda i: (i, 0))
    return call(
        input_grad_body,
        (length // rows,),
        [row(half)] * 6 + [full(w1.shape), full(w2.shape), row(width), row(width), full((1, width))],
        [row(width), full((8, width))],
        [jax.ShapeDtypeStruct((length, width), BF), jax.ShapeDtypeStruct((8, width), F32)],
        2 * length * width * half * 6,
        length * width * 20,
        name="input_grad",
    )(*grads1, *grads2, w1, w2, x, g_res, gain)


def per_device(
    layer_input,
    lengths,
    predicted,
    w_qkv,
    b_qkv,
    w_out,
    b_out,
    w_up,
    b_up,
    w_down,
    b_down,
    first_gain,
    first_bias,
    second_gain,
    second_bias,
    cotangent,
):
    own_seqs, length, width = layer_input.shape
    assert own_seqs == 1 and lax.axis_size("tensor") == 2
    swap = lambda v: lax.ppermute(v, "tensor", [(0, 1), (1, 0)])
    own_length = lax.dynamic_slice_in_dim(lengths, lax.axis_index("tensor"), 1, 0)
    x, ct = layer_input[0], cotangent[0]
    row = lambda v: v.astype(F32)[None, :]
    cosine, sine = (jnp.asarray(t) for t in rope_tables(length))

    w_qkv2 = swap(w_qkv)
    b_qkv2, w_out2, w_up2, b_up2, w_down2 = (swap(v) for v in (b_qkv, w_out, w_up, b_up, w_down))

    normed, *qkv1 = project(
        x, row(first_gain), row(first_bias), w_qkv, b_qkv.astype(F32), cosine, sine, True
    )
    e1, ot1, o1, linv1 = attend(own_length, *qkv1)
    qkv2 = project(normed, None, None, w_qkv2, b_qkv2.astype(F32), cosine, sine, False)
    e2, ot2, o2, linv2 = attend(own_length, *qkv2)
    residual, normed_two = out_project(
        o1, o2, w_out, w_out2, x, row(b_out), row(second_gain), row(second_bias)
    )
    dwu2, dwd2, dbu2, ff, dn = mlp(normed_two, ct, w_up2, row(b_up2), w_down2)
    dwu1, dwd1, dbu1, y, g_res, ga, vec2 = mlp(
        normed_two, ct, w_up, row(b_up), w_down, (ff, dn, residual, row(b_down), row(second_gain))
    )
    dmt2, dwo2 = mixed_grad(w_out2, ot2, ga)
    dmt1, dwo1 = mixed_grad(w_out, ot1, ga)
    grads2 = attend_grad(e2, linv2, *qkv2, ot2, dmt2, cosine, sine)
    dwq2, dbq2 = weight_grad(normed, grads2)
    grads1 = attend_grad(e1, linv1, *qkv1, ot1, dmt1, cosine, sine)
    dwq1, dbq1 = weight_grad(normed, grads1)
    input_grad, vec1 = input_gradient(grads1, grads2, w_qkv, w_qkv2, x, g_res, row(first_gain))

    def total(own, other):
        return lax.psum(own + swap(other), "dp").astype(F32)

    grad_w_up = total(dwu1, dwu2)
    grad_w_down = total(dwd1, dwd2)
    grad_w_out = total(dwo1, dwo2)
    grad_w_qkv = total(dwq1, dwq2)
    grad_b_qkv = total(dbq1, dbq2)
    grad_b_up = total(dbu1, dbu2)[0]

    classes = jnp.arange(CLASSES)
    valid = jnp.arange(length)[None, :] < own_length
    hits = (predicted == classes[:, None]) & valid
    counts = jnp.sum(hits.astype(F32), axis=1)
    vec, counts = lax.psum((jnp.concatenate([vec1[:2], vec2[:4]]), counts), ("dp", "tensor"))
    total_tokens = length * 2 * lax.axis_size("dp")
    return (
        y[None],
        input_grad[None],
        grad_w_qkv,
        grad_b_qkv,
        grad_w_out,
        vec[4],
        grad_w_up,
        grad_b_up,
        grad_w_down,
        vec[5],
        vec[0],
        vec[1],
        vec[2],
        vec[3],
        counts * (CLASSES / total_tokens),
    )


def solution(mesh):
    placed = (
        P(("dp", "tensor"), None, None),
        P("dp"),
        P(("dp", "tensor"), None),
        P(None, None, "tensor"),
        P(None, "tensor"),
        P("tensor", None),
        P(),
        P(None, "tensor"),
        P("tensor"),
        P("tensor", None),
        P(),
        P(),
        P(),
        P(),
        P(),
        P(("dp", "tensor"), None, None),
    )
    return jax.shard_map(
        per_device,
        mesh=mesh,
        in_specs=placed,
        out_specs=(
            P(("dp", "tensor"), None, None),
            P(("dp", "tensor"), None, None),
            P(None, None, "tensor"),
            P(None, "tensor"),
            P("tensor", None),
            P(),
            P(None, "tensor"),
            P("tensor"),
            P("tensor", None),
            P(),
            P(),
            P(),
            P(),
            P(),
            P(),
        ),
        check_vma=False,
    )
```

```python
import functools

import jax
import jax.numpy as jnp
import numpy as np
from jax import lax
from jax.experimental import pallas as pl
from jax.experimental.pallas import tpu as pltpu
from jax.sharding import PartitionSpec as P

HEAD_DIM = 64
CLASSES = 70
EPSILON = 1e-05
PAIR = 2 * HEAD_DIM
BF = jnp.bfloat16
F32 = jnp.float32
NN = (((1,), (0,)), ((), ()))
NT = (((1,), (1,)), ((), ()))
VMEM_LIMIT = 60 * 1024 * 1024

ERF_P = 0.39
ERF_C = (
    0.2353350342991649,
    0.09132489362337098,
    0.6497226730753285,
    -0.6356086817390623,
    0.886796488962974,
    -0.22757041290383279,
)


def dot(a, b, dims):
    return lax.dot_general(a, b, dims, preferred_element_type=F32)


def call(body, grid, in_specs, out_specs, out_shape, flops, nbytes, scratch=(), name=None):
    return pl.pallas_call(
        body,
        grid=grid,
        in_specs=in_specs,
        out_specs=out_specs,
        out_shape=out_shape,
        scratch_shapes=list(scratch),
        compiler_params=pltpu.CompilerParams(vmem_limit_bytes=VMEM_LIMIT),
        cost_estimate=pl.CostEstimate(
            flops=int(flops), bytes_accessed=int(nbytes), transcendentals=0
        ),
        name=name,
    )


def rope_tables(length):
    half = HEAD_DIM // 2
    freq = np.float32(10000.0) ** (-2.0 * np.arange(half).astype(np.float32) / np.float32(HEAD_DIM))
    angles = np.arange(length).astype(np.float32)[:, None] * freq.astype(np.float32)[None, :]
    cosine = np.cos(angles)
    sine = np.sin(angles)
    cosine = np.concatenate([cosine, cosine, cosine, cosine], axis=1)
    sine = np.concatenate([-sine, sine, -sine, sine], axis=1)
    return cosine.astype(np.float32), sine.astype(np.float32)


def turn(v):
    lane = lax.broadcasted_iota(jnp.int32, v.shape, 1)
    first = lax.rem(lane, HEAD_DIM) < HEAD_DIM // 2
    half = HEAD_DIM // 2
    return jnp.where(first, pltpu.roll(v, PAIR - half, 1), pltpu.roll(v, half, 1))


def ln_forward(x):
    centred = x - jnp.mean(x, axis=-1, keepdims=True)
    scale = lax.rsqrt(jnp.mean(centred * centred, axis=-1, keepdims=True) + EPSILON)
    return centred * scale, scale


def ln_backward(xhat, scale, grad, gain):
    h = grad * gain
    mean_h = jnp.mean(h, axis=-1, keepdims=True)
    mean_hx = jnp.mean(h * xhat, axis=-1, keepdims=True)
    return scale * (h - mean_h - xhat * mean_hx)


def full(shape):
    zeros = (0,) * len(shape)
    return pl.BlockSpec(shape, lambda *_: zeros)


def project_body(normalize, *refs):
    if normalize:
        x_ref, par_ref, w_ref, bias_ref, cos_ref, sin_ref, n_ref, q_ref, k_ref, v_ref = refs
        xhat, _ = ln_forward(x_ref[...].astype(F32))
        normed = (xhat * par_ref[0:1, :] + par_ref[1:2, :]).astype(BF)
        n_ref[...] = normed
    else:
        n_ref, w_ref, bias_ref, cos_ref, sin_ref, q_ref, k_ref, v_ref = refs
        normed = n_ref[...]
    cosine, sine = cos_ref[...], sin_ref[...]
    width = w_ref.shape[2]
    for c, out in ((0, q_ref), (1, k_ref), (2, v_ref)):
        y = dot(normed, w_ref[c], NN) + bias_ref[c : c + 1, :].astype(F32)
        if c == 2:
            out[...] = y.astype(BF)
            continue
        for p in range(width // PAIR):
            piece = y[:, p * PAIR : (p + 1) * PAIR]
            piece = piece * cosine + turn(piece) * sine
            if c == 0:
                piece = piece * (HEAD_DIM**-0.5)
            out[:, p * PAIR : (p + 1) * PAIR] = piece.astype(BF)


def project(x, params, w, b, cosine, sine):
    length, width = x.shape
    half = w.shape[2]
    rows = 256
    normalize = params is not None
    row = lambda n: pl.BlockSpec((rows, n), lambda i: (i, 0))
    head = [x, params] if normalize else [x]
    head_specs = [row(width)] + ([full(params.shape)] if normalize else [])
    outs = [jax.ShapeDtypeStruct((length, half), BF)] * 3
    out_specs = [row(half)] * 3
    if normalize:
        outs = [jax.ShapeDtypeStruct((length, width), BF)] + outs
        out_specs = [row(width)] + out_specs
    return call(
        functools.partial(project_body, normalize),
        (length // rows,),
        head_specs + [full(w.shape), full(b.shape), row(PAIR), row(PAIR)],
        out_specs,
        outs,
        2 * length * width * half * 3,
        2 * (length * width * 2 + 3 * width * half + 3 * length * half),
        name="project",
    )(*head, w, b, cosine, sine)


def attend_body(len_ref, q_ref, k_ref, v_ref, e_ref, ot_ref, o_ref, linv_ref):
    length = q_ref.shape[0]
    step = 256
    valid = lax.broadcasted_iota(jnp.int32, (length, PAIR), 0) < len_ref[0]
    lane = lax.broadcasted_iota(jnp.int32, (length, PAIR), 1)
    q, k = q_ref[...], k_ref[...]
    v_t = jnp.transpose(v_ref[...])
    ones = jnp.ones((16, length), BF)
    mask = jnp.where(valid, 0.0, -1.0e9).astype(BF)
    work = []
    for h in range(2):
        other = HEAD_DIM * (1 - h)
        own = (lane >= HEAD_DIM * h) & (lane < HEAD_DIM * (h + 1))
        q_h = jnp.where(own, q, jnp.where(lane == other, 1.0, 0.0).astype(BF))
        k_h = jnp.where(lane == other, mask, k)
        v_h = jnp.concatenate([v_t[HEAD_DIM * h : HEAD_DIM * (h + 1)], ones], axis=0)
        for c in range(length // step):
            work.append((h, c, q_h, k_h, v_h))

    def scores(item):
        h, c, q_h, k_h, v_h = item
        return dot(k_h, q_h[c * step : (c + 1) * step], NT)

    ahead = scores(work[0])
    for i, item in enumerate(work):
        h, c, q_h, k_h, v_h = item
        now = ahead
        if i + 1 < len(work):
            ahead = scores(work[i + 1])
        where = slice(c * step, (c + 1) * step)
        top = jnp.max(now, axis=0, keepdims=True)
        e = jnp.exp(now - top).astype(BF)
        e_ref[h, :, where] = e
        o = dot(v_h, e, NN)
        linv = 1.0 / o[HEAD_DIM : HEAD_DIM + 1]
        linv_ref[0, h : h + 1, where] = linv
        ot_ref[HEAD_DIM * h : HEAD_DIM * (h + 1), where] = (o[:HEAD_DIM] * linv).astype(BF)
    o_ref[...] = jnp.transpose(ot_ref[...])


def attend(own_length, q, k, v):
    length, half = q.shape
    pairs = half // PAIR
    col = pl.BlockSpec((length, PAIR), lambda p: (0, p))
    return call(
        attend_body,
        (pairs,),
        [pl.BlockSpec(memory_space=pltpu.SMEM), col, col, col],
        [
            pl.BlockSpec((2, length, length), lambda p: (p, 0, 0)),
            pl.BlockSpec((PAIR, length), lambda p: (p, 0)),
            col,
            pl.BlockSpec((1, 8, length), lambda p: (p, 0, 0)),
        ],
        [
            jax.ShapeDtypeStruct((2 * pairs, length, length), BF),
            jax.ShapeDtypeStruct((half, length), BF),
            jax.ShapeDtypeStruct((length, half), BF),
            jax.ShapeDtypeStruct((pairs, 8, length), F32),
        ],
        2 * 4 * length * length * PAIR * pairs,
        4 * pairs * length * length,
        name="attend",
    )(own_length, q, k, v)


def attend_grad_body(
    e_ref, linv_ref, q_ref, k_ref, v_ref, ot_ref, dot_ref, cos_ref, sin_ref, dq_ref, dk_ref, dv_ref
):
    length = q_ref.shape[0]
    step = 256
    lane = lax.broadcasted_iota(jnp.int32, (length, PAIR), 1)
    q, v = q_ref[...], v_ref[...]
    k_t = jnp.transpose(k_ref[...])
    zeros = jnp.zeros((HEAD_DIM, length), BF)
    work = []
    for h in range(2):
        rows = slice(HEAD_DIM * h, HEAD_DIM * (h + 1))
        own = (lane >= HEAD_DIM * h) & (lane < HEAD_DIM * (h + 1))
        q_h = jnp.where(own, q, jnp.zeros_like(q))
        d_o = dot_ref[rows, :].astype(F32) * linv_ref[0, h : h + 1, :]
        delta = jnp.sum(d_o * ot_ref[rows, :].astype(F32), axis=0, keepdims=True)
        d_low = d_o.astype(BF)
        d_pad = jnp.concatenate([d_low, zeros] if h == 0 else [zeros, d_low], axis=0)
        for c in range(length // step):
            work.append((h, c, q_h, d_pad, delta, k_t[rows]))

    def grad_probs(item):
        h, c, q_h, d_pad, delta, k_h = item
        return dot(v, d_pad[:, c * step : (c + 1) * step], NN)

    d_v = jnp.zeros((length, PAIR), F32)
    d_k = jnp.zeros((length, PAIR), F32)
    d_q = [[], []]
    ahead = grad_probs(work[0])
    for i, item in enumerate(work):
        h, c, q_h, d_pad, delta, k_h = item
        now = ahead
        if i + 1 < len(work):
            ahead = grad_probs(work[i + 1])
        where = slice(c * step, (c + 1) * step)
        e = e_ref[h, :, where]
        d_s = (e.astype(F32) * (now - delta[:, where])).astype(BF)
        d_v = d_v + dot(e, d_pad[:, where], NT)
        d_k = d_k + dot(d_s, q_h[where], NN)
        d_q[h].append(dot(k_h, d_s, NN))
    cosine, sine = cos_ref[...], sin_ref[...]
    dv_ref[...] = d_v.astype(BF)
    dk_ref[...] = (d_k * cosine - turn(d_k) * sine).astype(BF)
    both = [jnp.concatenate(parts, axis=1) for parts in d_q]
    both = jnp.transpose(jnp.concatenate(both, axis=0)) * (HEAD_DIM**-0.5)
    dq_ref[...] = (both * cosine - turn(both) * sine).astype(BF)


def attend_grad(pair, e, linv, q, k, v, o_t, do_t, cosine, sine):
    length = q.shape[0]
    col = pl.BlockSpec((length, PAIR), lambda p: (0, pair))
    row = pl.BlockSpec((PAIR, length), lambda p: (pair, 0))
    return call(
        attend_grad_body,
        (1,),
        [
            pl.BlockSpec((2, length, length), lambda p: (pair, 0, 0)),
            pl.BlockSpec((1, 8, length), lambda p: (pair, 0, 0)),
            col,
            col,
            col,
            row,
            row,
            full((length, PAIR)),
            full((length, PAIR)),
        ],
        [full((length, PAIR))] * 3,
        [jax.ShapeDtypeStruct((length, PAIR), BF)] * 3,
        2 * 8 * length * length * PAIR,
        4 * length * length,
        name="attend_grad",
    )(e, linv, q, k, v, o_t, do_t, cosine, sine)


def out_body(o1_ref, o2_ref, w1_ref, w2_ref, x_ref, par_ref, res_ref, n_ref):
    res = dot(o1_ref[...], w1_ref[...], NN) + dot(o2_ref[...], w2_ref[...], NN)
    res = x_ref[...].astype(F32) + (res + par_ref[2:3, :])
    res_ref[...] = res
    xhat, _ = ln_forward(res)
    n_ref[...] = (xhat * par_ref[3:4, :] + par_ref[4:5, :]).astype(BF)


def out_project(o1, o2, w1, w2, x, params):
    length, width = x.shape
    half = w1.shape[0]
    rows = 256
    row = lambda n: pl.BlockSpec((rows, n), lambda i: (i, 0))
    return call(
        out_body,
        (length // rows,),
        [row(half), row(half), full(w1.shape), full(w2.shape), row(width), full(params.shape)],
        [row(width)] * 2,
        [jax.ShapeDtypeStruct((length, width), F32), jax.ShapeDtypeStruct((length, width), BF)],
        2 * length * width * half * 2,
        length * width * 10,
        name="out_project",
    )(o1, o2, w1, w2, x, params)


def gelu_parts(u):
    z = jnp.abs(u) * (0.5**0.5)
    t = 1.0 / (1.0 + ERF_P * z)
    poly = jnp.full_like(t, ERF_C[-1])
    for coef in ERF_C[-2::-1]:
        poly = poly * t + coef
    e = jnp.exp(u * u * -0.5)
    tail = 0.5 * (poly * t) * e
    cdf = jnp.where(u >= 0, 1.0 - tail, tail)
    return u * cdf, cdf + u * (e * 0.3989422804014327)


def mlp_body(last, *refs):
    if last:
        (n_ref, ct_ref, wu_ref, bu_ref, wd_ref, ff_in, dn_in, res_ref, par_ref) = refs[:9]
        (dw_ref, dbu_ref, y_ref, gres_ref, gat_ref, vec_ref) = refs[9:15]
        (ff_ref, dn_ref, nt_ref, ctt_ref) = refs[15:]
    else:
        n_ref, ct_ref, wu_ref, bu_ref, wd_ref = refs[:5]
        dw_ref, dbu_ref, ff_ref, dn_ref, nt_ref, ctt_ref = refs[5:]
    j = pl.program_id(0)

    @pl.when(j == 0)
    def _():
        nt_ref[...] = jnp.transpose(n_ref[...])
        ctt_ref[...] = jnp.transpose(ct_ref[...])
        if last:
            ff_ref[...] = ff_in[...]
            dn_ref[...] = dn_in[...]
        else:
            ff_ref[...] = jnp.zeros_like(ff_ref)
            dn_ref[...] = jnp.zeros_like(dn_ref)

    n, ct, wu, wd = n_ref[...], ct_ref[...], wu_ref[...], wd_ref[...]
    up = dot(n, wu, NN) + bu_ref[...]
    d_act = dot(ct, wd, NT)
    act, slope = gelu_parts(up)
    act = act.astype(BF)
    d_up = (d_act * slope).astype(BF)
    ff_ref[...] += dot(act, wd, NN)
    width = nt_ref.shape[0]
    dw_ref[0, width:, :] = dot(ctt_ref[...], act, NN).astype(BF)
    dw_ref[0, :width, :] = dot(nt_ref[...], d_up, NN).astype(BF)
    dn_ref[...] += dot(d_up, wu, NT)
    dbu_ref[...] = jnp.sum(d_up.astype(F32), axis=0, keepdims=True)

    if last:

        @pl.when(j == pl.num_programs(0) - 1)
        def _():
            length = n_ref.shape[0]
            step = 128
            vec_ref[...] = jnp.zeros_like(vec_ref)

            def tail(i, carry):
                at = pl.ds(pl.multiple_of(i * step, step), step)
                res = res_ref[at, :]
                y_ref[at, :] = (res + (ff_ref[at, :] + par_ref[5:6, :])).astype(BF)
                xhat, scale = ln_forward(res)
                d_n = dn_ref[at, :]
                c = ct_ref[at, :].astype(F32)
                g_res = c + ln_backward(xhat, scale, d_n, par_ref[3:4, :])
                gres_ref[at, :] = g_res
                low = g_res.astype(BF)
                gat_ref[:, at] = jnp.transpose(low)
                vec_ref[0:1, :] += jnp.sum(d_n * xhat, axis=0, keepdims=True)
                vec_ref[1:2, :] += jnp.sum(d_n, axis=0, keepdims=True)
                vec_ref[2:3, :] += jnp.sum(low.astype(F32), axis=0, keepdims=True)
                vec_ref[3:4, :] += jnp.sum(c, axis=0, keepdims=True)
                return carry

            lax.fori_loop(0, length // step, tail, 0)


def mlp(n, ct, wu, bu, wd, rest=None):
    length, width = n.shape
    half = wu.shape[1]
    block = half // 3
    last = rest is not None
    whole = full((length, width))
    bias = pl.BlockSpec((1, block), lambda j: (0, j))
    in_specs = [
        whole,
        whole,
        pl.BlockSpec((width, block), lambda j: (0, j)),
        bias,
        pl.BlockSpec((block, width), lambda j: (j, 0)),
    ]
    args = [n, ct, wu, bu, wd]
    outs = [
        jax.ShapeDtypeStruct((3, 2 * width, block), BF),
        jax.ShapeDtypeStruct((1, half), F32),
    ]
    out_specs = [pl.BlockSpec((1, 2 * width, block), lambda j: (j, 0, 0)), bias]
    big = jax.ShapeDtypeStruct((length, width), F32)
    low = jax.ShapeDtypeStruct((length, width), BF)
    scratch = [pltpu.VMEM((width, length), BF)] * 2
    if last:
        args += list(rest)
        in_specs += [whole, whole, whole, full((8, width))]
        outs += [low, big, jax.ShapeDtypeStruct((width, length), BF)]
        outs += [jax.ShapeDtypeStruct((8, width), F32)]
        out_specs += [whole, whole, full((width, length)), full((8, width))]
        scratch = [pltpu.VMEM((length, width), F32)] * 2 + scratch
    else:
        outs += [big, big]
        out_specs += [whole, whole]
    return call(
        functools.partial(mlp_body, last),
        (half // block,),
        in_specs,
        out_specs,
        outs,
        2 * length * width * half * 6,
        length * width * 20 + 8 * width * half,
        scratch,
        name="mlp_last" if last else "mlp_first",
    )(*args)


def mixed_grad_body(w_ref, o_ref, gat_ref, dm_ref, dw_ref):
    gat = gat_ref[...]
    dm_ref[...] = dot(w_ref[...], gat, NN).astype(BF)
    dw_ref[...] = dot(gat, o_ref[...], NN).astype(BF)


def mixed_grad(w, o, gat):
    half, width = w.shape
    length = gat.shape[1]
    return call(
        mixed_grad_body,
        (1,),
        [full(w.shape), full(o.shape), full(gat.shape)],
        [full((half, length)), full((width, half))],
        [jax.ShapeDtypeStruct((half, length), BF), jax.ShapeDtypeStruct((width, half), BF)],
        4 * length * width * half,
        2 * (2 * half * length + length * width + 2 * half * width),
        name="mixed_grad",
    )(w, o, gat)


def weight_grad_body(n_ref, dwo_ref, *refs):
    grads, (dw_ref, db_ref, nt_ref) = refs[:-3], refs[-3:]
    width = n_ref.shape[1]
    third = width // 3
    pairs = len(grads) // 3
    nt_ref[...] = jnp.transpose(n_ref[...])
    for c in range(3):
        d = jnp.concatenate([grads[3 * p + c][...] for p in range(pairs)], axis=1)
        dw_ref[c, :width, :] = dot(nt_ref[...], d, NN).astype(BF)
        dw_ref[c, width:, :] = dwo_ref[c * third : (c + 1) * third, :]
        db_ref[c : c + 1, :] = jnp.sum(d.astype(F32), axis=0, keepdims=True)


def weight_grad(n, dwo, grads):
    length, width = n.shape
    half = dwo.shape[1]
    rows = width + width // 3
    return call(
        weight_grad_body,
        (1,),
        [full(n.shape), full(dwo.shape)] + [full((length, PAIR))] * len(grads),
        [full((3, rows, half)), full((3, half))],
        [jax.ShapeDtypeStruct((3, rows, half), BF), jax.ShapeDtypeStruct((3, half), F32)],
        2 * length * width * half * 3,
        2 * (length * width + 3 * length * half + 3 * width * half),
        [pltpu.VMEM((width, length), BF)],
        name="weight_grad",
    )(n, dwo, *grads)


def input_grad_body(*refs):
    grads, (w1_ref, w2_ref, x_ref, gres_ref, par_ref), (out_ref, vec_ref) = (
        refs[:-7],
        refs[-7:-2],
        refs[-2:],
    )
    pairs = len(grads) // 6
    d_n = None
    for i, w_ref in enumerate((w1_ref, w2_ref)):
        for c in range(3):
            mine = grads[3 * pairs * i : 3 * pairs * (i + 1)]
            d = jnp.concatenate([mine[3 * p + c][...] for p in range(pairs)], axis=1)
            term = dot(d, w_ref[c], NT)
            d_n = term if d_n is None else d_n + term
    xhat, scale = ln_forward(x_ref[...].astype(F32))
    out_ref[...] = (gres_ref[...] + ln_backward(xhat, scale, d_n, par_ref[0:1, :])).astype(BF)

    @pl.when(pl.program_id(0) == 0)
    def _():
        vec_ref[...] = jnp.zeros_like(vec_ref)

    vec_ref[0:1, :] += jnp.sum(d_n * xhat, axis=0, keepdims=True)
    vec_ref[1:2, :] += jnp.sum(d_n, axis=0, keepdims=True)


def input_gradient(grads, w1, w2, x, g_res, params):
    length, width = x.shape
    half = w1.shape[2]
    rows = 256
    row = lambda n: pl.BlockSpec((rows, n), lambda i: (i, 0))
    return call(
        input_grad_body,
        (length // rows,),
        [row(PAIR)] * len(grads)
        + [full(w1.shape), full(w2.shape), row(width), row(width), full(params.shape)],
        [row(width), full((8, width))],
        [jax.ShapeDtypeStruct((length, width), BF), jax.ShapeDtypeStruct((8, width), F32)],
        2 * length * width * half * 6,
        length * width * 20,
        name="input_grad",
    )(*grads, w1, w2, x, g_res, params)


COLORS = 3


def bit_orders(count):
    bits = list(range(count.bit_length() - 1))
    lead = bits[:COLORS]
    return [lead[c:] + lead[:c] + bits[COLORS:] for c in range(COLORS)]


def exchange(v, bit):
    count = lax.axis_size("dp")
    return lax.ppermute(v, "dp", [(i, i ^ (1 << bit)) for i in range(count)])


def split_body(keep_ref, *refs):
    ins, outs = refs[: 4 * COLORS], refs[4 * COLORS :]
    for c in range(COLORS):
        for part in range(2):
            a, b = ins[4 * c + 2 * part][...], ins[4 * c + 2 * part + 1][...]
            total = (a.astype(F32) + b.astype(F32)).astype(BF)
            outs[2 * c + part][...] = total.reshape(outs[2 * c + part].shape)


def split_sum(keep, first, second):
    joint = first[0].ndim == 4
    pieces, rows, cols = first[0].shape[-3:]
    half = pieces // 2
    block = max(1, half // 4)
    ins, in_specs, out_specs = [], [], []

    def spec(c, kept):
        def index(i, keep_ref):
            mine = keep_ref[c]
            which = mine if kept else 1 - mine
            return (c if joint else 0, which, i, 0, 0)

        return pl.BlockSpec((1, 1, block, rows, cols), index)

    for c in range(COLORS):
        for kept in (False, True):
            for source in (first, second):
                a = source[0] if joint else source[c]
                ins.append(a.reshape(-1, 2, half, rows, cols))
                in_specs.append(spec(c, kept))
            out_specs.append(pl.BlockSpec((block, rows, cols), lambda i, keep_ref: (i, 0, 0)))
    out = jax.ShapeDtypeStruct((half, rows, cols), BF)
    outs = pl.pallas_call(
        split_body,
        grid_spec=pltpu.PrefetchScalarGridSpec(
            num_scalar_prefetch=1,
            grid=(half // block,),
            in_specs=in_specs,
            out_specs=out_specs,
        ),
        out_shape=[out] * (2 * COLORS),
        compiler_params=pltpu.CompilerParams(vmem_limit_bytes=VMEM_LIMIT),
        cost_estimate=pl.CostEstimate(
            flops=COLORS * pieces * rows * cols,
            bytes_accessed=COLORS * pieces * rows * cols * 6,
            transcendentals=0,
        ),
        name="split_sum",
    )(keep, *ins)
    return outs[0::2], outs[1::2]


def add_body(*refs):
    for c in range(COLORS):
        a, b = refs[c][...], refs[COLORS + c][...]
        refs[2 * COLORS + c][...] = (a.astype(F32) + b.astype(F32)).astype(BF)


def join_body(*refs):
    for c in range(COLORS):
        a, b, out = refs[c], refs[COLORS + c], refs[2 * COLORS + c]
        count = a.shape[0]
        out[:count] = a[...]
        out[count:] = b[...]


def combine(body, first, second, grow, name):
    count, rows, cols = first[0].shape
    out = (count * grow, rows, cols)
    return call(
        body,
        (1,),
        [full(first[0].shape)] * (2 * COLORS),
        [full(out)] * COLORS,
        [jax.ShapeDtypeStruct(out, BF)] * COLORS,
        COLORS * count * rows * cols,
        COLORS * count * rows * cols * 8,
        name=name,
    )(*first, *second)


def piece_order(count):
    me = lax.axis_index("dp")
    bits, places = [], []
    for order in bit_orders(count):
        mine = [(me >> b) & 1 for b in order]
        place = mine[0]
        for bit in mine[1:]:
            place = place * 2 + bit
        bits.append(mine)
        places.append(place)
    keeps = [jnp.stack([bits[c][s] for c in range(COLORS)]) for s in range(len(bits[0]))]
    return [k.astype(jnp.int32) for k in keeps], jnp.stack(places).astype(jnp.int32)


def dp_sum(own, other, keeps):
    count = lax.axis_size("dp")
    orders = bit_orders(count)
    steps = len(keeps)
    colors, rows, cols = own.shape
    shape = (colors, count, rows // count, cols)
    first, second = [own.reshape(shape)], [other.reshape(shape)]
    for s in range(steps):
        send, first = split_sum(keeps[s], first, second)
        second = [exchange(v, orders[c][s]) for c, v in enumerate(send)]
    held = combine(add_body, first, second, 1, "add_last")
    for s in reversed(range(steps)):
        got = [exchange(v, orders[c][s]) for c, v in enumerate(held)]
        if s:
            held = combine(join_body, held, got, 2, "join")
    return held, got


def place_body(split, place_ref, *refs):
    near, far = refs[:COLORS], refs[COLORS : 2 * COLORS]
    straight_ref, turned_ref, scratch = refs[2 * COLORS :]
    half, rows, cols = near[0].shape
    color = pl.program_id(0)
    for c in range(COLORS):

        @pl.when(color == c)
        def _():
            place = place_ref[c]
            for p in range(2 * half):
                relative = p ^ place
                at = relative & (half - 1)
                piece = jnp.where(relative < half, near[c][at], far[c][at]).astype(F32)
                if p < split:
                    target = pl.ds(p * rows, rows)
                    if len(straight_ref.shape) == 3:
                        straight_ref[0, target, :] = piece
                    else:
                        straight_ref[target, :] = piece
                else:
                    scratch[(p - split) * rows : (p - split + 1) * rows, :] = piece
            turned_ref[...] = jnp.transpose(scratch[...])


def place_pieces(places, near, far, split, straight, straight_spec, turned, turned_spec):
    half, rows, cols = near[0].shape
    size = COLORS * 2 * half * rows * cols
    return pl.pallas_call(
        functools.partial(place_body, split),
        grid_spec=pltpu.PrefetchScalarGridSpec(
            num_scalar_prefetch=1,
            grid=(COLORS,),
            in_specs=[pl.BlockSpec((half, rows, cols), lambda c, _: (0, 0, 0))] * (2 * COLORS),
            out_specs=[straight_spec, turned_spec],
            scratch_shapes=[pltpu.VMEM(((2 * half - split) * rows, cols), F32)],
        ),
        out_shape=[jax.ShapeDtypeStruct(straight, F32), jax.ShapeDtypeStruct(turned, F32)],
        compiler_params=pltpu.CompilerParams(vmem_limit_bytes=VMEM_LIMIT),
        cost_estimate=pl.CostEstimate(flops=size, bytes_accessed=size * 6, transcendentals=0),
        name="place_pieces",
    )(places, *near, *far)


def weight_sums(own, other, keeps, places, width, wide):
    count = lax.axis_size("dp")
    colors, rows, cols = own.shape
    turned_rows = rows - width
    if count & (count - 1) or (rows // count) % 16 or width % (rows // count):
        total = lax.psum(own + other, "dp").astype(F32)
        straight, turned = total[:, :width], total[:, width:]
        turned = jnp.transpose(turned, (0, 2, 1))
        if wide:
            straight = jnp.transpose(straight, (1, 0, 2)).reshape(width, colors * cols)
            return straight, turned.reshape(colors * cols, turned_rows)
        return straight, jnp.transpose(turned, (1, 0, 2)).reshape(cols, colors * turned_rows)
    near, far = dp_sum(own, other, keeps)
    split = width // (rows // count)
    if wide:
        return place_pieces(
            places, near, far, split,
            (width, colors * cols), pl.BlockSpec((width, cols), lambda c, _: (0, c)),
            (colors * cols, turned_rows), pl.BlockSpec((cols, turned_rows), lambda c, _: (c, 0)),
        )
    return place_pieces(
        places, near, far, split,
        (colors, width, cols), pl.BlockSpec((1, width, cols), lambda c, _: (c, 0, 0)),
        (cols, colors * turned_rows), pl.BlockSpec((cols, turned_rows), lambda c, _: (0, c)),
    )


def per_device(
    layer_input,
    lengths,
    predicted,
    w_qkv,
    b_qkv,
    w_out,
    b_out,
    w_up,
    b_up,
    w_down,
    b_down,
    first_gain,
    first_bias,
    second_gain,
    second_bias,
    cotangent,
):
    own_seqs, length, width = layer_input.shape
    assert own_seqs == 1 and lax.axis_size("tensor") == 2
    swap = lambda v: lax.ppermute(v, "tensor", [(0, 1), (1, 0)])
    own_length = lax.dynamic_slice_in_dim(lengths, lax.axis_index("tensor"), 1, 0)
    x, ct = layer_input[0], cotangent[0]
    count = lax.axis_size("dp")
    cosine, sine = (jnp.asarray(t) for t in rope_tables(length))

    w_qkv2 = swap(w_qkv)
    b_qkv2, w_out2, w_up2, b_up2, w_down2 = (swap(v) for v in (b_qkv, w_out, w_up, b_up, w_down))
    vectors = (first_gain, first_bias, b_out, second_gain, second_bias, b_down)
    params = jnp.pad(jnp.stack(vectors).astype(F32), ((0, 2), (0, 0)))
    keeps, places = piece_order(count)

    normed, *qkv1 = project(x, params, w_qkv, b_qkv, cosine, sine)
    e1, ot1, o1, linv1 = attend(own_length, *qkv1)
    qkv2 = project(normed, None, w_qkv2, b_qkv2, cosine, sine)
    e2, ot2, o2, linv2 = attend(own_length, *qkv2)
    residual, normed_two = out_project(o1, o2, w_out, w_out2, x, params)
    dmlp2, dbu2, ff, dn = mlp(normed_two, ct, w_up2, b_up2.astype(F32)[None], w_down2)
    dmlp1, dbu1, y, g_res, gat, vec2 = mlp(
        normed_two, ct, w_up, b_up.astype(F32)[None], w_down, (ff, dn, residual, params)
    )
    grad_w_up, grad_w_down = weight_sums(dmlp1, swap(dmlp2), keeps, places, width, True)

    dmt2, dwo2 = mixed_grad(w_out2, o2, gat)
    dmt1, dwo1 = mixed_grad(w_out, o1, gat)
    pairs = w_out.shape[0] // PAIR
    tables = (cosine, sine)
    grads2, grads1 = [], []
    for p in range(pairs):
        grads2 += attend_grad(p, e2, linv2, *qkv2, ot2, dmt2, *tables)
    dqkv2, dbq2 = weight_grad(normed, dwo2, grads2)
    for p in range(pairs):
        grads1 += attend_grad(p, e1, linv1, *qkv1, ot1, dmt1, *tables)
    dqkv1, dbq1 = weight_grad(normed, dwo1, grads1)
    grad_w_qkv, grad_w_out = weight_sums(dqkv1, swap(dqkv2), keeps, places, width, False)
    input_grad, vec1 = input_gradient(grads1 + grads2, w_qkv, w_qkv2, x, g_res, params)

    classes = jnp.arange(CLASSES)
    valid = jnp.arange(length)[None, :] < own_length
    hits = (predicted == classes[:, None]) & valid
    counts = jnp.pad(jnp.sum(hits.astype(F32), axis=1), (0, width - CLASSES))
    shared = jnp.concatenate([vec1[:2], vec2[:4], counts[None]])
    half_rows = lambda dbu, dbq: jnp.concatenate(
        [dbu.reshape(-1, width), jnp.pad(dbq, ((0, 0), (0, width - dbq.shape[1])))]
    )
    small = jnp.concatenate([shared, half_rows(dbu1, dbq1)])
    small = small + swap(jnp.concatenate([shared, half_rows(dbu2, dbq2)]))
    if count & (count - 1):
        small = lax.psum(small, "dp")
    else:
        for bit in range(count.bit_length() - 1):
            small = small + exchange(small, bit)
    up_rows = dbu1.shape[1] // width
    total_tokens = length * 2 * count
    return (
        y[None],
        input_grad[None],
        grad_w_qkv,
        small[7 + up_rows :, : dbq1.shape[1]],
        grad_w_out,
        small[4],
        grad_w_up,
        small[7 : 7 + up_rows].reshape(-1),
        grad_w_down,
        small[5],
        small[0],
        small[1],
        small[2],
        small[3],
        small[6, :CLASSES] * (CLASSES / total_tokens),
    )


def solution(mesh):
    placed = (
        P(("dp", "tensor"), None, None),
        P("dp"),
        P(("dp", "tensor"), None),
        P(None, None, "tensor"),
        P(None, "tensor"),
        P("tensor", None),
        P(),
        P(None, "tensor"),
        P("tensor"),
        P("tensor", None),
        P(),
        P(),
        P(),
        P(),
        P(),
        P(("dp", "tensor"), None, None),
    )
    return jax.shard_map(
        per_device,
        mesh=mesh,
        in_specs=placed,
        out_specs=(
            P(("dp", "tensor"), None, None),
            P(("dp", "tensor"), None, None),
            P(None, None, "tensor"),
            P(None, "tensor"),
            P("tensor", None),
            P(),
            P(None, "tensor"),
            P("tensor"),
            P("tensor", None),
            P(),
            P(),
            P(),
            P(),
            P(),
            P(),
        ),
        check_vma=False,
    )
```
